256 devices in a mesh: replica: 16 (over y_lo, x, core), shard: 16 (over y_hi, z).
Axes of the slice: x: 4, y: 4 (y_hi: 2, y_lo: 2; y = y_hi * 2 + y_lo), z: 8, core: 2. Of those that a mesh axis runs over, the one named last changes fastest.
Arguments:
- grads: bfloat16 [16, 16, 256, 8192], P('replica', 'shard'), may hold values from -1.25 to 1.25
- master: float32 [256, 8192], P('shard'), may hold values from -0.003 to 0.003
- moment_one: float32 [256, 8192], P('shard'), may hold values from -0.75 to 0.75
- moment_two: float32 [256, 8192], P('shard'), may hold values from 0.005 to 0.2
Outputs:
- master_out: float32 [256, 8192], P('shard')
- moment_one_out: float32 [256, 8192], P('shard')
- moment_two_out: float32 [256, 8192], P('shard')
- weights: bfloat16 [256, 8192], replicated
The draws below stay inside these ranges and needn't reach their ends.
All inputs are finite; a program needn't handle non-finite values.
Results may differ from the reference program's by a relative error of at most 0.012.
Values may be sent and summed in bfloat16 or wider, within the bound.
No kernel may reach another device: no remote copies, remote signals or barrier semaphores. Data moves between devices by JAX's collectives and lax.ppermute only.
A program may use at most 64 MiB of HBM per device.

```python
import math
import jax
import jax.numpy as jnp
from jax import lax

D = 8192
ROWS = 256
STEP = 20
N_REPLICA = 16
N_SHARD = 16


def spiked(values, stream_key, source, target, parts, factor):
    def block_of(dim):
        return (jnp.arange(values.shape[dim]) // (values.shape[dim] // parts)).reshape((-1,) + (1,) * (values.ndim - 1 - dim))

    one_side = jax.random.permutation(stream_key, parts)[block_of(target)]
    far = (block_of(target) + parts // 2) % parts
    return jnp.where((block_of(source) == one_side) | (block_of(source) == far), factor * values, values)


def levels(rng, dims, pieces, least, largest):
    gain, own = 1.0, jax.random.fold_in(rng, 6)
    for position, blocks in pieces:
        heights = jnp.exp(jax.random.uniform(jax.random.fold_in(own, position), (blocks,), jnp.float32, least / len(pieces), largest / len(pieces)))
        gain = gain * jnp.repeat(heights, dims[position] // blocks).reshape([-1 if axis == position else 1 for axis in range(len(dims))])
    return gain


def gaussian(stream_key, extent, spread, reach, split=(), dtype=jnp.bfloat16):
    level = levels(stream_key, extent, split, -0.22, 0.18) if split else 1.0
    entries = jax.random.normal(stream_key, extent, jnp.float32) * spread * level
    return jnp.minimum(jnp.maximum(entries, -reach), reach).astype(dtype)


def bell_draw_with(key, extent, scale, limit, shards, heavy, dtype=jnp.bfloat16):
    result = scale * jax.random.normal(key, extent, jnp.float32)
    if shards:
        result = result * levels(key, extent, shards, -0.22, 0.18)
    return jnp.clip(spiked(result, jax.random.fold_in(key, 3), *heavy), -limit, limit).astype(dtype)


def setup_inputs(seed: int = 0) -> dict:
    streams_of = jax.random.split(jax.random.key(seed), 5)
    grads = bell_draw_with(streams_of[0], (N_REPLICA, N_SHARD, ROWS, D), 0.0625, 1.25, ((0, 16), (1, 16)), (1, 2, 16, 2.0))
    master = jnp.clip(jax.random.uniform(streams_of[1], (ROWS, D), jnp.float32, -0.003, 0.003) * levels(streams_of[1], (ROWS, D), ((0, 16),), -0.4, 0.0), -0.003, 0.003)
    moment_one = gaussian(streams_of[2], (ROWS, D), 0.05, 0.75, ((0, 16),), jnp.float32)
    moment_two = jnp.clip(jnp.exp(math.log(0.2) - 3.6888795 * jax.random.uniform(streams_of[3], (ROWS, D), jnp.float32) ** levels(streams_of[3], (ROWS, D), ((0, 16),), -0.2, 0.2)), 0.005, 0.2)
    return dict(grads=grads, master=master, moment_one=moment_one, moment_two=moment_two)


def adam_update(total, master, moment_one, moment_two):
    first = 0.9 * moment_one + 0.1 * total
    second = 0.95 * moment_two + 0.05 * total * total
    first_hat = first / (1.0 - 0.9 ** STEP)
    second_hat = second / (1.0 - 0.95 ** STEP)
    updated = master - 0.0003 * (first_hat / (jnp.sqrt(second_hat) + 1e-08) + 0.1 * master)
    return (updated, first, second)

def reference(grads, master, moment_one, moment_two):

    def add_replica(carry, block):
        return (carry + lax.optimization_barrier(jnp.sum(block.astype(jnp.float32), axis=0)), None)
    total, unused = lax.scan(add_replica, jnp.zeros((ROWS, D), jnp.float32), grads)
    updated, first, second = adam_update(total, master, moment_one, moment_two)
    return (updated, first, second, updated.astype(jnp.bfloat16))
```

```python
import jax
import jax.numpy as jnp
from jax import lax
from jax.sharding import PartitionSpec as P

STEP = 20
AXES = ("replica", "shard")
BF = jnp.bfloat16
F32 = jnp.float32
U32 = jnp.uint32


def adam_update(total, master, moment_one, moment_two):
    first = 0.9 * moment_one + 0.1 * total
    second = 0.95 * moment_two + 0.05 * total * total
    first_hat = first / (1.0 - 0.9**STEP)
    second_hat = second / (1.0 - 0.95**STEP)
    updated = master - 0.0003 * (first_hat / (jnp.sqrt(second_hat) + 1e-08) + 0.1 * master)
    return (updated, first, second)


def flat(x, y, z, c):
    return ((y % 2) * 8 + x * 2 + c) * 16 + (y // 2) * 8 + z


def pairs(move):
    return [
        (flat(x, y, z, c), flat(*move(x, y, z, c)))
        for x in range(4)
        for y in range(4)
        for z in range(8)
        for c in range(2)
    ]


def send(value, move):
    return lax.ppermute(value, AXES, pairs(move))


def core(value):
    return send(value, lambda x, y, z, c: (x, y, z, 1 - c))


def along_x(value, k):
    return send(value, lambda x, y, z, c: ((x + k) % 4, y, z, c))


def along_y(value, k):
    return send(value, lambda x, y, z, c: (x, (y + k) % 4, z, c))


def cut(value, row, col, rows, cols):
    row, col = jnp.asarray(row, U32), jnp.asarray(col, U32)
    return lax.dynamic_slice(value, (row, col), (rows, cols))


def put(whole, value, row, col):
    row, col = jnp.asarray(row, U32), jnp.asarray(col, U32)
    return lax.dynamic_update_slice(whole, value, (row, col))


def add(values):
    total = values[0].astype(F32)
    for value in values[1:]:
        total = total + value.astype(F32)
    return total


def local(grads, master, moment_one, moment_two):
    g = grads[0, 0]
    r = lax.axis_index("replica").astype(U32)
    s = lax.axis_index("shard").astype(U32)
    yl, x, c = r >> 3, (r >> 1) & 3, r & 1
    yh = s >> 3
    y = yh * 2 + yl
    half, far = c * 4096, (1 - c) * 4096
    z_groups = [list(range(8)), list(range(8, 16))]

    def a_at(t):
        return U32(0), t * 512

    def b_at(t):
        return (t >> 1) * 128, 2048 + (t & 1) * 1024

    mine_a, mine_b = {}, {}
    for k in (2, 1, 3, 0):
        row, col = a_at((x + k) & 3)
        got = core(cut(g, row, far + col, 256, 512))
        mine_a[k] = add([cut(g, row, half + col, 256, 512), got]).astype(BF)
        row, col = b_at((y + k) & 3)
        got = core(cut(g, row, far + col, 128, 1024))
        mine_b[k] = add([cut(g, row, half + col, 128, 1024), got]).astype(BF)
    got_a = {k: along_x(mine_a[k], k) for k in (2, 1, 3)}
    got_b = {k: along_y(mine_b[k], k) for k in (2, 1, 3)}
    a = add([mine_a[0], got_a[1], got_a[3], got_a[2]]).astype(BF)
    b = add([mine_b[0], got_b[1], got_b[3], got_b[2]]).astype(BF)

    def a2(t):
        return cut(a, (t >> 1) * 128, (t & 1) * 256, 128, 256)

    def b2(t):
        return cut(b, 0, t * 256, 128, 256)

    got_a = {k: along_y(a2((y + k) & 3), k) for k in (2, 1, 3)}
    got_b = {k: along_x(b2((x + k) & 3), k) for k in (2, 1, 3)}
    a = add([a2(y), got_a[1], got_a[3], got_a[2]]).astype(BF)
    b = add([b2(x), got_b[1], got_b[3], got_b[2]]).astype(BF)
    ab = jnp.concatenate([a, b], axis=1).reshape(8, 16, 512)
    ab = lax.all_to_all(ab, "shard", 0, 0, tiled=True, axis_index_groups=z_groups)
    piece = add([ab[i] for i in range(8)]).astype(BF)

    a_col = half + x * 512 + yl * 256
    b_col = half + 2048 + yl * 1024 + x * 256

    def own(v):
        return jnp.concatenate([cut(v, 0, a_col, 16, 256), cut(v, 0, b_col, 16, 256)], axis=1)

    w = adam_update(piece.astype(F32), own(master), own(moment_one), own(moment_two))[0].astype(BF)
    w = lax.all_to_all(
        jnp.broadcast_to(w[None], (8, 16, 512)), "shard", 0, 0, tiled=True, axis_index_groups=z_groups
    ).reshape(128, 512)
    a, b = w[:, :256], w[:, 256:]
    wa = jnp.zeros((256, 512), BF)
    wb = jnp.zeros((128, 1024), BF)
    for k in (0, 1, 3, 2):
        t = (y + 4 - k) & 3
        wa = put(wa, along_y(a, k) if k else a, (t >> 1) * 128, (t & 1) * 256)
        t = (x + 4 - k) & 3
        wb = put(wb, along_x(b, k) if k else b, 0, t * 256)
    weights = jnp.zeros((256, 8192), BF)
    for k in (0, 1, 3, 2):
        piece_a = along_x(wa, k) if k else wa
        row, col = a_at((x + 4 - k) & 3)
        weights = put(weights, piece_a, row, half + col)
        weights = put(weights, core(piece_a), row, far + col)
        piece_b = along_y(wb, k) if k else wb
        row, col = b_at((y + 4 - k) & 3)
        weights = put(weights, piece_b, row, half + col)
        weights = put(weights, core(piece_b), row, far + col)

    rows = lax.all_to_all(jnp.broadcast_to(piece[None], (16, 16, 512)), "replica", 0, 0, tiled=True)
    rows = rows.reshape(2, 4, 2, 16, 2, 256)
    rows_a = rows[:, :, :, :, 0].transpose(3, 2, 1, 0, 4).reshape(16, 2, 2048)
    rows_b = rows[:, :, :, :, 1].transpose(3, 2, 0, 1, 4).reshape(16, 2, 2048)
    total = jnp.concatenate([rows_a, rows_b], axis=2).reshape(16, 8192).astype(F32)
    updated, first, second = adam_update(total, master, moment_one, moment_two)
    return (updated, first, second, weights)


def solution(mesh):
    placed = (
        P("replica", "shard", None, None),
        P("shard", None),
        P("shard", None),
        P("shard", None),
    )
    return jax.shard_map(
        local,
        mesh=mesh,
        in_specs=placed,
        out_specs=(P("shard", None), P("shard", None), P("shard", None), P()),
        check_vma=False,
    )
```

```python
import jax
import jax.numpy as jnp
from jax import lax
from jax.experimental import pallas as pl
from jax.sharding import PartitionSpec as P


STEP = 20
AXES = ("replica", "shard")
BF = jnp.bfloat16
F32 = jnp.float32
U32 = jnp.uint32


def adam_update(total, master, moment_one, moment_two):
    first = 0.9 * moment_one + 0.1 * total
    second = 0.95 * moment_two + 0.05 * total * total
    first_hat = first / (1.0 - 0.9**STEP)
    second_hat = second / (1.0 - 0.95**STEP)
    updated = master - 0.0003 * (first_hat / (jnp.sqrt(second_hat) + 1e-08) + 0.1 * master)
    return (updated, first, second)


def flat(x, y, z, c):
    return ((y % 2) * 8 + x * 2 + c) * 16 + (y // 2) * 8 + z


def send(value, move):
    pairs = [
        (flat(x, y, z, c), flat(*move(x, y, z, c)))
        for x in range(4)
        for y in range(4)
        for z in range(8)
        for c in range(2)
    ]
    return lax.ppermute(value, AXES, pairs)


def over_core(value):
    return send(value, lambda x, y, z, c: (x, y, z, 1 - c))


def along_a(value, k):
    return send(value, lambda x, y, z, c: ((x + k) % 4, y, z, c) if c == 0 else (x, (y + k) % 4, z, c))


def along_b(value, k):
    return send(value, lambda x, y, z, c: (x, (y + k) % 4, z, c) if c == 0 else ((x + k) % 4, y, z, c))


def tiles(value):
    rows, cols = value.shape
    return value.reshape(rows // 8, 8, cols // 128, 128).transpose(0, 2, 1, 3)


def untiles(value):
    rt, ct = value.shape[:2]
    return value.transpose(0, 2, 1, 3).reshape(rt * 8, ct * 128)


def cut(value, starts, sizes):
    starts = [jnp.asarray(i, U32) for i in starts] + [U32(0)] * (value.ndim - len(starts))
    return lax.dynamic_slice(value, starts, tuple(sizes) + value.shape[len(sizes) :])


def put(whole, value, starts):
    starts = [jnp.asarray(i, U32) for i in starts] + [U32(0)] * (whole.ndim - len(starts))
    return lax.dynamic_update_slice(whole, value, starts)


def unset(shape, dtype):
    return pl.pallas_call(
        lambda out: None, out_shape=jax.ShapeDtypeStruct(shape, dtype), out_specs=pl.BlockSpec(memory_space=pl.ANY)
    )()


def add(values):
    total = values[0].astype(F32)
    for value in values[1:]:
        total = total + value.astype(F32)
    return total.astype(BF)


def local(grads, master, moment_one, moment_two):
    g = tiles(grads[0, 0])
    r = lax.axis_index("replica").astype(U32)
    s = lax.axis_index("shard").astype(U32)
    yl, x, c = r >> 3, (r >> 1) & 3, r & 1
    yh = s >> 3
    y = yh * 2 + yl
    core1 = c == 1
    a_pos, a_far = jnp.where(core1, y, x), jnp.where(core1, x, y)
    b_pos = jnp.where(core1, x, y)
    z_groups = [list(range(8)), list(range(8, 16))]

    def block(core_is_1, base, t, j):
        row = jnp.where(core_is_1, t >> 1, U32(j)) * 16
        col = jnp.where(core_is_1, 2 * (t & 1) + j, t) * 8
        return row, base + col

    half, far = c * 32, (1 - c) * 32
    states = [tiles(v) for v in (master, moment_one, moment_two)]
    col = half + jnp.where(core1, yl * 16 + x * 4, x * 8 + yl * 4)
    own_states = [cut(v, (0, col), (2, 4)) for v in states]

    def quarter(value, core_is_1, base, t):
        halves = cut(value, ((t >> 1) * 16, base + (t & 1) * 16), (16, 16)).reshape(256, 8, 128)
        columns = cut(value, (0, base + t * 8), (32, 8)).reshape(256, 8, 128)
        return jnp.where(core_is_1, halves, columns)

    def outgoing(source, k):
        return quarter(source, c == 0, far, (a_far + k) & 3)

    def merged(own, got, k):
        return add([quarter(own, core1, U32(0), (a_pos + k) & 3), got])

    out, g = lax.optimization_barrier((outgoing(g, 2), g))
    sent = {2: over_core(out)}
    own, g = lax.optimization_barrier((cut(g, (0, half), (32, 32)), g))
    mine = {2: merged(own, sent[2], 2)}
    mine[2], g, own = lax.optimization_barrier((mine[2], g, own))
    out = {k: outgoing(g, k) for k in (1, 3, 0)}
    for k in (1, 3, 0):
        sent[k] = over_core(out[k])
    for k in (1, 3, 0):
        mine[k], own = lax.optimization_barrier((merged(own, sent[k], k), own))
    got = {k: along_a(mine[k], k) for k in (2, 1, 3)}
    sums = add([mine[0], got[1], got[3], got[2]])

    def part(t):
        rows = cut(sums.reshape(32, 8, 8, 128), ((t >> 1) * 16, (t & 1) * 4), (16, 4))
        return jnp.where(core1, cut(sums.reshape(16, 16, 8, 128), (0, t * 4), (16, 4)), rows)

    got = {k: along_b(part((b_pos + k) & 3), k) for k in (2, 1, 3)}
    sums = add([part(b_pos), got[1], got[3], got[2]])
    sums, own_states = lax.optimization_barrier((sums, own_states))
    sums = lax.all_to_all(sums.reshape(8, 2, 4, 8, 128), "shard", 0, 0, tiled=True, axis_index_groups=z_groups)
    piece = add([sums[i] for i in range(8)])

    w = adam_update(piece.astype(F32), *own_states)[0].astype(BF)
    other = over_core(piece)
    w = lax.all_to_all(
        jnp.broadcast_to(w[None], (8, 2, 4, 8, 128)), "shard", 0, 0, tiled=True, axis_index_groups=z_groups
    ).reshape(16, 4, 8, 128)
    whole = unset((2, 16, 8, 8, 128), BF)
    for k in (0, 1, 3, 2):
        t = (b_pos + 4 - k) & 3
        whole = put(whole, (along_b(w, k) if k else w)[None], (t >> 1, 0, (t & 1) * 4))
    got = {k: along_a(whole, k) for k in (2, 1, 3)}
    got[0] = whole
    weights = unset((32, 64, 8, 128), BF)
    for k in (0, 1, 3, 2):
        for j in (0, 1):
            weights = put(weights, got[k][j], block(core1, half, (a_pos + 4 - k) & 3, j))
        theirs = over_core(got[k])
        for j in (0, 1):
            weights = put(weights, theirs[j], block(c == 0, far, (a_far + 4 - k) & 3, j))

    rows = jnp.stack([jnp.where(core1, other, piece), jnp.where(core1, piece, other)])
    other = send(rows, lambda x, y, z, c: (x, y ^ 1, z, c))
    rows = jnp.stack([jnp.where(yl == 1, other, rows), jnp.where(yl == 1, rows, other)])
    moved = {k: send(rows, lambda x, y, z, c, k=k: ((x + k) % 4, y, z, c)) for k in (2, 1, 3)}
    moved[0] = rows
    total = unset((4, 2, 2, 2, 4, 8, 128), BF)
    for k in (0, 1, 3, 2):
        total = put(total, moved[k][None], ((x + 4 - k) & 3,))
    total0 = total[:, :, 0].transpose(2, 0, 1, 3, 4, 5).reshape(2, 32, 8, 128)
    total1 = total[:, :, 1].transpose(2, 1, 0, 3, 4, 5).reshape(2, 32, 8, 128)
    total = jnp.concatenate([total0, total1], axis=1).astype(F32)
    out = adam_update(total, *states)
    return (*[untiles(v) for v in out], untiles(weights))


def solution(mesh):
    placed = (
        P("replica", "shard", None, None),
        P("shard", None),
        P("shard", None),
        P("shard", None),
    )
    return jax.shard_map(
        local,
        mesh=mesh,
        in_specs=placed,
        out_specs=(P("shard", None), P("shard", None), P("shard", None), P()),
        check_vma=False,
    )
```
